128 devices in a mesh: context: 32 (over z, y, core), tensor: 4 (over x).
Axes of the slice: x: 4, y: 4, z: 4, core: 2. Of those that a mesh axis runs over, the one named last changes fastest.
Arguments:
- hidden: bfloat16 [1024, 4096], P('context', 'tensor'), may hold values from -270 to 270
- weight: bfloat16 [4096, 128256], P(None, ('context', 'tensor')), may hold values from -0.25 to 0.25
- targets: int32 [1024], P('context'), may hold values from 0 to 128255
- mask: int32 [1024], P('context'), may hold values 0 or 1
- loss_scale: float32 [], replicated, may hold values from 2048 to 32768
Outputs:
- loss: float32 [], replicated
- grad_hidden: bfloat16 [1024, 4096], P('context', 'tensor')
- grad_weight: bfloat16 [4096, 128256], P(None, ('context', 'tensor'))
The draws below stay inside these ranges and needn't reach their ends.
All inputs are finite; a program needn't handle non-finite values. No bound on the sum of `mask` on one device may be relied on, other than what follows from the above.
Results may differ from the reference program's by a relative error of at most 0.0052.
Values may be sent and summed in bfloat16 or wider, within the bound.
A program may use at most 128 MiB of HBM per device.

```python
import math
import jax
import jax.numpy as jnp
import numpy as np
from jax import lax

D = 4096
V = 128256
TOKENS = 1024


def draw_hidden(key, part):
    keys = jax.random.split(jax.random.fold_in(key, 11), 1)
    base = jnp.clip(jax.random.normal(keys[0], (TOKENS, D), jnp.float32), -6.0, 6.0)
    values = base
    return values.astype(jnp.bfloat16)


def touch_ends(values, stream_key, low, top_value):
    longest = values.shape.index(max(values.shape))
    spots = []
    for shift in (0, 1):
        where = [jax.random.randint(jax.random.fold_in(stream_key, axis), (), 0, length) for axis, length in enumerate(values.shape)]
        where[longest] = (where[longest] + shift) % values.shape[longest]
        spots.append(tuple(where))
    return values.at[spots[0]].set(low).at[spots[1]].set(top_value)


def block_scale(rng, dims, pieces, smallest, top_value):
    gain = 1.0
    for axis_at, parts in pieces:
        heights = jax.random.uniform(jax.random.fold_in(jax.random.fold_in(rng, 6), axis_at), (parts,), jnp.float32, smallest / len(pieces), top_value / len(pieces))
        gain = gain * jnp.repeat(jnp.exp(heights), dims[axis_at] // parts).reshape((-1,) + (1,) * (len(dims) - 1 - axis_at))
    return gain


def skewed_wide(own_key, extent, amount, skew):
    weights = [min(1 << octave, amount + 1 - (1 << octave)) * (1 << 20) // math.isqrt((1 << octave) ** skew) + 1 for octave in range((amount + 1).bit_length()) if 1 << octave <= amount]
    spread = 1 + sum(weights) // (1 << 30)
    grid = np.cumsum(np.array([max(1, weight // spread) for weight in weights]))
    ticket = jax.random.randint(jax.random.fold_in(own_key, 1), extent, 0, int(grid[len(weights) - 1]))
    start = jnp.left_shift(1, jnp.searchsorted(jnp.asarray(grid, jnp.int32), ticket, side="right").astype(jnp.int32))
    grade = start - 1 + jax.random.randint(jax.random.fold_in(own_key, 4), extent, 0, 1 << 30) % jnp.minimum(start, amount + 1 - start)
    return jax.random.permutation(jax.random.fold_in(own_key, 2), amount)[grade].astype(jnp.int32)


def noise(stream_key, shape, deviation, limit, cuts=(), kind=jnp.bfloat16):
    drawn = deviation * jax.random.normal(stream_key, shape, jnp.float32)
    if cuts:
        drawn = drawn * block_scale(stream_key, shape, cuts, -0.22, 0.18)
    return jnp.clip(drawn, -limit, limit).astype(kind)


def setup_inputs(seed: int = 0) -> dict:
    splits = jax.random.split(jax.random.key(seed), 6)
    return {
        "hidden": draw_hidden(jax.random.fold_in(splits[5], 71), 0),
        "weight": noise(splits[1], (D, V), (D // 9) ** -0.5, 0.25, ((1, 128),)),
        "targets": touch_ends(skewed_wide(splits[2], (TOKENS,), V, 2), jax.random.fold_in(splits[2], 3), 0, V - 1).astype(jnp.int32),
        "mask": touch_ends((jax.random.randint(splits[3], (TOKENS,), 0, 4) < 3).astype(jnp.int32), jax.random.fold_in(splits[3], 1), 0, 1),
        "loss_scale": jnp.clip(jnp.exp(jax.random.uniform(splits[4], (), jnp.float32, math.log(2048.0), math.log(32768.0))), 2048.0, 32768.0),
    }


clip_limit = 1.0

def reference(hidden, weight, targets, mask, loss_scale):
    logits = jnp.dot(hidden, weight, preferred_element_type=jnp.float32)
    row_max = lax.optimization_barrier(jnp.max(logits, axis=1))
    shifted = jnp.exp(logits - row_max[:, None])
    sum_exp = lax.optimization_barrier(jnp.sum(shifted, axis=1))
    target_logit = jnp.take_along_axis(logits, targets.astype(jnp.int32)[:, None], axis=1)[:, 0]
    token_loss = jnp.log(sum_exp) + row_max - target_logit
    maskf = mask.astype(jnp.float32)
    denom = jnp.maximum(jnp.sum(maskf), jnp.float32(1.0))
    loss = jnp.sum(maskf * token_loss) / denom
    columns = lax.broadcasted_iota(jnp.int32, (1, logits.shape[1]), 1)
    onehot = (columns == targets.astype(jnp.int32)[:, None]).astype(jnp.float32)
    factor = loss_scale * maskf / denom
    grad_logits = (factor[:, None] * (shifted / sum_exp[:, None] - onehot)).astype(jnp.bfloat16)
    grad_hidden = lax.dot_general(grad_logits, weight, (((1,), (1,)), ((), ())), preferred_element_type=jnp.float32).astype(jnp.bfloat16)
    raw_grad = lax.dot_general(hidden, grad_logits, (((0,), (0,)), ((), ())), preferred_element_type=jnp.float32)
    grad_norm = jnp.sqrt(jnp.sum(raw_grad * raw_grad)) / loss_scale
    grad_weight = (raw_grad * (clip_limit / jnp.maximum(grad_norm, clip_limit))).astype(jnp.bfloat16)
    return (loss, grad_hidden, grad_weight)
```

```python
import jax
import jax.numpy as jnp
from jax import lax
from jax.experimental import pallas as pl
from jax.experimental.pallas import tpu as pltpu
from jax.sharding import Mesh
from jax.sharding import PartitionSpec as P

CONTEXT = ("context_0", "context_1", "context_2")
CONTEXT_TENSOR = ("context_0", "context_1", "context_2", "tensor")
MESH_ID = pl.DeviceIdType.MESH

AXIS = {"x": "tensor", "y": "context_1", "z": "context_0", "c": "context_2"}
PARTS = ((0, 384, "xyz"), (384, 384, "yzx"), (768, 256, "zxy"))
ROWS = 32
WIDE = 1024
VOCAB = 1002
EDGE = 1000
PAD = 1024
TOKENS = 1024
ALL = slice(None)
LO, HI, BOTH = pl.ds(0, 16), pl.ds(16, 16), pl.ds(0, 32)
N_SEMS = 160

clip_limit = 1.0


def kernel(
    hidden_ref, weight_ref, edge_ref, targets_ref, mask_ref, scale_ref,
    loss_ref, clip_ref, gh_ref, raw_ref,
    hid, wgt, soft, dlt, dl, give, take, own, t3, r3, t2, r2, t1, r1, tm, st, ss, stage,
    send_sem, recv_sem, local_sem,
):
    f32, bf16 = jnp.float32, jnp.bfloat16
    me = {k: lax.axis_index(a) for k, a in AXIS.items()}
    up = {k: lax.rem(me[k] + 1, 4) for k in "xyz"}
    down = {k: lax.rem(me[k] + 3, 4) for k in "xyz"}
    far = {k: lax.rem(me[k] + 2, 4) for k in "xyz"}
    core, sib = me["c"], 1 - me["c"]
    used = [0]
    sent = []

    def copy(src, dst, dim, to):
        k = used[0]
        used[0] += 1
        c = pltpu.make_async_remote_copy(
            src_ref=src, dst_ref=dst, send_sem=send_sem.at[k], recv_sem=recv_sem.at[k],
            device_id={AXIS[dim]: to}, device_id_type=MESH_ID,
        )
        c.start()
        sent.append(c)
        return c

    load_w = pltpu.make_async_copy(
        weight_ref.at[pl.ds(0, EDGE)], wgt.at[pl.ds(0, EDGE)], local_sem.at[0]
    )
    load_w.start()
    mine = pltpu.make_async_copy(
        hidden_ref, hid.at[me["x"], core, me["z"], me["y"]], local_sem.at[1]
    )
    mine.start()
    own_tm = tm.at[core, me["z"], me["y"]]
    own_tm[...] = jnp.zeros((8, 128), jnp.int32)
    own_tm[0:1, 0:ROWS] = targets_ref[...]
    own_tm[1:2, 0:ROWS] = mask_ref[...]

    keep = lax.broadcasted_iota(jnp.int32, (8, 4 * WIDE), 0) < VOCAB - EDGE
    edge = jnp.where(keep, edge_ref[...].astype(f32), 0.0)
    rest = jnp.zeros((PAD - EDGE - 8, 4 * WIDE), f32)
    wgt[EDGE:PAD, :] = jnp.concatenate([edge, rest], axis=0).astype(bf16)

    barrier = pltpu.get_barrier_semaphore()
    peers = [(d, where[d]) for d in "xyz" for where in (up, down, far)] + [("c", sib)]
    for dim, to in peers:
        pl.semaphore_signal(barrier, inc=1, device_id={AXIS[dim]: to}, device_id_type=MESH_ID)
    pl.semaphore_wait(barrier, len(peers))
    mine.wait()

    def hview(part, s, v, rows):
        off, w, order = PARTS[part]
        at = {d: (ALL if i < s else (v if i == s else me[d])) for i, d in enumerate(order)}
        return hid.at[at["x"], core, at["z"], at["y"], rows, pl.ds(off, w)]

    def swap(dim, views, to):
        return copy(views, views, dim, to)

    def gather_start(part, s):
        d = PARTS[part][2][s]
        lo, hi = hview(part, s, me[d], LO), hview(part, s, me[d], HI)
        a = swap(d, lo, up[d])
        b = swap(d, hi, down[d])
        e = swap(d, hi, up[d])
        f = swap(d, lo, down[d])
        return a, b, e, f

    def gather_pass(part, s, cs):
        d = PARTS[part][2][s]
        cs[0].wait_recv()
        g = swap(d, hview(part, s, down[d], LO), up[d])
        cs[1].wait_recv()
        h = swap(d, hview(part, s, up[d], HI), down[d])
        return g, h

    fwd = []

    def forward(part, s, v):
        view = hview(part, s, v, BOTH)
        fwd.append(swap("c", view, sib))

    three = (0, 1, 2)
    tcs = [copy(own_tm, own_tm, "c", sib)]
    for s in three:
        started = [gather_start(p, s) for p in three]
        passed = [gather_pass(p, s, started[p]) for p in three]
        if s == 0:
            tcs[0].wait_recv()
            view = tm.at[:, me["z"], me["y"]]
            tcs = [copy(view, view, "y", where["y"]) for where in (up, down, far)]
        if s == 1:
            for t in tcs:
                t.wait_recv()
            view = tm.at[:, me["z"]]
            tcs = [copy(view, view, "z", where["z"]) for where in (up, down, far)]
        for p in three:
            d = PARTS[p][2][s]
            started[p][2].wait_recv()
            if s == 2:
                forward(p, s, down[d])
            started[p][3].wait_recv()
            if s == 2:
                forward(p, s, up[d])
        for p in three:
            d = PARTS[p][2][s]
            passed[p][0].wait_recv()
            passed[p][1].wait_recv()
            if s == 2:
                forward(p, s, far[d])
            if s == 1:
                forward(p, 2, me[PARTS[p][2][2]])
    for t in tcs:
        t.wait_recv()
    load_w.wait()
    for t in fwd:
        t.wait_recv()

    def by_token(row):
        groups = []
        for c in range(2):
            for z in range(4):
                total = tm[c, z, 0, row : row + 1, :]
                for y in range(1, 4):
                    total = total + pltpu.roll(tm[c, z, y, row : row + 1, :], ROWS * y, 1)
                groups.append(total)
        return jnp.concatenate(groups, axis=1)

    targets = by_token(0)
    maskf = by_token(1).astype(f32)

    @pl.loop(0, 4)
    def _(n):
        c, z = n // 2, 2 * lax.rem(n, 2)
        cols = pl.ds(pl.multiple_of(n * 256, 256), 256)
        for x in range(4):
            rows = hid[x, c, pl.ds(z, 2)].reshape(256, WIDE)
            part = lax.dot_general(
                wgt[:, x * WIDE : (x + 1) * WIDE], rows, (((1,), (1,)), ((), ())),
                preferred_element_type=f32,
            )
            if x == 0:
                soft[:, cols] = part
            else:
                soft[:, cols] += part

    place = ((me["z"] * 4 + me["y"]) * 2 + core) * 4 + me["x"]
    first = place * VOCAB
    vocab_row = lax.broadcasted_iota(jnp.int32, (PAD, 128), 0)
    real = vocab_row < VOCAB
    for n in range(8):
        cols = slice(n * 128, (n + 1) * 128)
        logits = jnp.where(real, soft[:, cols], -jnp.inf)
        top = jnp.max(logits, axis=0, keepdims=True)
        e = jnp.exp(logits - top)
        soft[:, cols] = e
        hit = (vocab_row == targets[:, cols] - first) & real
        st[0, core, 0, :, cols] = top
        st[0, core, 1, :, cols] = jnp.sum(e, axis=0, keepdims=True)
        st[0, core, 2, :, cols] = jnp.sum(jnp.where(hit, logits, 0.0), axis=0, keepdims=True)
    local_top = st[0, core, 0]

    def others(d):
        return (("c", sib),) if d == "c" else tuple((d, w[d]) for w in (up, down, far))

    for i, d in enumerate("cxyz"):
        view = st.at[i, me[d]]
        cs = [copy(view, view, dim, to) for dim, to in others(d)]
        for c in cs:
            c.wait_recv()
        n = 2 if d == "c" else 4
        tops = [st[i, k, 0] for k in range(n)]
        top = tops[0]
        for k in range(1, n):
            top = jnp.maximum(top, tops[k])
        total = st[i, 0, 1] * jnp.exp(tops[0] - top)
        target = st[i, 0, 2]
        for k in range(1, n):
            total = total + st[i, k, 1] * jnp.exp(tops[k] - top)
            target = target + st[i, k, 2]
        if i < 3:
            nxt = me["cxyz"[i + 1]]
            st[i + 1, nxt, 0] = top
            st[i + 1, nxt, 1] = total
            st[i + 1, nxt, 2] = target

    loss_scale = scale_ref[0, 0]
    denom = jnp.maximum(jnp.sum(maskf, keepdims=True), 1.0)
    token_loss = jnp.log(total) + top - target
    loss = jnp.sum(maskf * token_loss, keepdims=True) / denom
    loss_ref[...] = jnp.broadcast_to(loss, (8, 128))
    factor = loss_scale * maskf / denom
    ratio = jnp.exp(local_top - top) / total

    for n in range(8):
        cols = slice(n * 128, (n + 1) * 128)
        hit = (vocab_row == targets[:, cols] - first) & real
        g = factor[:, cols] * (soft[:, cols] * ratio[:, cols] - jnp.where(hit, 1.0, 0.0))
        g = jnp.where(real, g, 0.0)
        dlt[:, cols] = g.astype(bf16)
        dl[cols, :] = jnp.transpose(g).astype(bf16)

    def hidden_grad(part, half, add, out):
        off, w, _ = PARTS[part]
        rows = pl.ds(pl.multiple_of(half * 512, 512), 512)

        @pl.loop(0, 4)
        def _(x):
            cols = pl.ds(pl.multiple_of(x * WIDE + off, 128), w)
            r = jnp.dot(dl[rows, :], wgt[:, cols], preferred_element_type=f32)
            r = r.reshape(4, 4, ROWS, w)
            if add is not None:
                r = r + add[x, :, :, :, off : off + w].astype(f32)
            out[x, :, :, :, off : off + w] = r.astype(bf16)

    def whole(buf, part):
        off, w, _ = PARTS[part]
        return buf.at[:, :, :, :, pl.ds(off, w)]

    def gview(part, s, v, rows):
        off, w, order = PARTS[part]
        at = {d: (ALL if i < s else (v if i == s else me[d])) for i, d in enumerate(order)}
        return own.at[at["x"], at["z"], at["y"], rows, pl.ds(off, w)]

    def landing(bufs, k, part, s, rows):
        off, w, _ = PARTS[part]
        lead = (ALL,) * s
        return bufs.at[(k, *lead, rows, pl.ds(off, w))]

    spill = {2: (t3, r3), 1: (t2, r2), 0: (t1, r1)}

    def scatter_start(part, s):
        d = PARTS[part][2][s]
        t, r = spill[s]
        first16 = pl.ds(0, 16)
        return (
            copy(gview(part, s, far[d], LO), landing(t, 0, part, s, first16), d, up[d]),
            copy(gview(part, s, far[d], HI), landing(t, 1, part, s, first16), d, down[d]),
            copy(gview(part, s, up[d], HI), landing(r, 0, part, s, HI), d, up[d]),
            copy(gview(part, s, down[d], LO), landing(r, 1, part, s, LO), d, down[d]),
        )

    def scatter_pass(part, s, cs):
        d = PARTS[part][2][s]
        t, r = spill[s]
        first16 = pl.ds(0, 16)
        cs[0].wait_recv()
        v = gview(part, s, up[d], LO)
        v[...] = (v[...].astype(f32) + landing(t, 0, part, s, first16)[...].astype(f32)).astype(bf16)
        a = copy(v, landing(r, 0, part, s, LO), d, up[d])
        cs[1].wait_recv()
        v = gview(part, s, down[d], HI)
        v[...] = (v[...].astype(f32) + landing(t, 1, part, s, first16)[...].astype(f32)).astype(bf16)
        b = copy(v, landing(r, 1, part, s, HI), d, down[d])
        return a, b

    def scatter_end(part, s, cs, ps):
        d = PARTS[part][2][s]
        _, r = spill[s]
        for c in (cs[2], cs[3], *ps):
            c.wait_recv()
        v = gview(part, s, me[d], BOTH)
        total = (
            v[...].astype(f32)
            + landing(r, 0, part, s, BOTH)[...].astype(f32)
            + landing(r, 1, part, s, BOTH)[...].astype(f32)
        )
        if s > 0:
            v[...] = total.astype(bf16)
        else:
            off, w, _ = PARTS[part]
            gh_ref[:, off : off + w] = total.astype(bf16)

    pairs = []
    for p in three:
        hidden_grad(p, sib, None, give)
        pairs.append(copy(whole(give, p), whole(take, p), "c", sib))
    cs3, ps3 = [None] * 3, [None] * 3
    for p in three:
        pairs[p].wait_recv()
        hidden_grad(p, core, take, own)
        cs3[p] = scatter_start(p, 2)

    ss[0, core] = jnp.zeros((8, 128), f32)

    def weight_grad(first_step, steps):
        @pl.loop(first_step, first_step + steps)
        def _(n):
            x, h = n // 2, lax.rem(n, 2)
            cols = pl.ds(pl.multiple_of(h * 512, 512), 512)
            at = pl.ds(pl.multiple_of(n * 512, 512), 512)
            rows = hid[x, :, :, :, :, cols].reshape(TOKENS, 512)
            r = jnp.dot(dlt[...], rows, preferred_element_type=f32)
            sq = jnp.sum((r * r).reshape(PAD // 8, 8, 512), axis=0)
            ss[0, core] += sq[:, :128] + sq[:, 128:256] + sq[:, 256:384] + sq[:, 384:]
            slot = lax.rem(n, 2)

            @pl.when(n >= 2)
            def _():
                pltpu.make_async_copy(
                    stage.at[slot], raw_ref.at[:, at], local_sem.at[2 + slot]
                ).wait()

            stage[slot] = r[:VOCAB].astype(bf16)
            pltpu.make_async_copy(stage.at[slot], raw_ref.at[:, at], local_sem.at[2 + slot]).start()

    weight_grad(0, 3)
    ps3[0] = scatter_pass(0, 2, cs3[0])
    weight_grad(3, 1)
    ps3[1] = scatter_pass(1, 2, cs3[1])
    weight_grad(4, 1)
    ps3[2] = scatter_pass(2, 2, cs3[2])
    weight_grad(5, 3)
    ss[0, core] = jnp.broadcast_to(jnp.sum(ss[0, core], keepdims=True), (8, 128))

    def sum_start(i):
        d = "cxyz"[i]
        view = ss.at[i, me[d]]
        return [copy(view, view, dim, to) for dim, to in others(d)]

    def sum_end(i, cs):
        for c in cs:
            c.wait_recv()
        n = 2 if i == 0 else 4
        total = ss[i, 0]
        for k in range(1, n):
            total = total + ss[i, k]
        if i < 3:
            ss[i + 1, me["cxyz"[i + 1]]] = total
        return total

    q = sum_start(0)
    cs2, ps2, cs1, ps1 = [None] * 3, [None] * 3, [None] * 3, [None] * 3
    sum_end(0, q)
    q = sum_start(1)
    for p in (2, 0, 1):
        scatter_end(p, 2, cs3[p], ps3[p])
        cs2[p] = scatter_start(p, 1)
    sum_end(1, q)
    q = sum_start(2)
    for p in (2, 0, 1):
        ps2[p] = scatter_pass(p, 1, cs2[p])
    sum_end(2, q)
    q = sum_start(3)
    for p in (2, 0, 1):
        scatter_end(p, 1, cs2[p], ps2[p])
        cs1[p] = scatter_start(p, 0)
    squares = sum_end(3, q)
    for p in (2, 0, 1):
        ps1[p] = scatter_pass(p, 0, cs1[p])
    for p in (2, 0, 1):
        scatter_end(p, 0, cs1[p], ps1[p])
    norm = jnp.sqrt(squares) / loss_scale
    clip_ref[...] = clip_limit / jnp.maximum(norm, clip_limit)
    for slot in range(2):
        at = pl.ds((6 + slot) * 512, 512)
        pltpu.make_async_copy(stage.at[slot], raw_ref.at[:, at], local_sem.at[2 + slot]).wait()
    for c in sent:
        c.wait_send()


def step(hidden, weight, targets, mask, loss_scale):
    f32, bf16 = jnp.float32, jnp.bfloat16
    any_space = pl.BlockSpec(memory_space=pl.ANY)
    vmem = pl.BlockSpec(memory_space=pltpu.VMEM)
    smem = pl.BlockSpec(memory_space=pltpu.SMEM)
    V = pltpu.VMEM
    loss, clip, grad_hidden, raw = pl.pallas_call(
        kernel,
        out_shape=(
            jax.ShapeDtypeStruct((8, 128), f32),
            jax.ShapeDtypeStruct((8, 128), f32),
            jax.ShapeDtypeStruct((ROWS, WIDE), bf16),
            jax.ShapeDtypeStruct((VOCAB, 4 * WIDE), bf16),
        ),
        grid=(1,),
        in_specs=[
            any_space, any_space, pl.BlockSpec((8, 4 * WIDE), lambda i: (EDGE // 8, 0)), vmem, vmem, smem,
        ],
        out_specs=(vmem, vmem, vmem, any_space),
        scratch_shapes=[
            V((4, 2, 4, 4, ROWS, WIDE), bf16),
            V((PAD, 4 * WIDE), bf16),
            V((PAD, TOKENS), f32),
            V((PAD, TOKENS), bf16),
            V((TOKENS, PAD), bf16),
            V((4, 4, 4, ROWS, WIDE), bf16),
            V((4, 4, 4, ROWS, WIDE), bf16),
            V((4, 4, 4, ROWS, WIDE), bf16),
            V((2, 4, 4, 16, WIDE), bf16),
            V((2, 4, 4, ROWS, WIDE), bf16),
            V((2, 4, 16, WIDE), bf16),
            V((2, 4, ROWS, WIDE), bf16),
            V((2, 16, WIDE), bf16),
            V((2, ROWS, WIDE), bf16),
            V((2, 4, 4, 8, 128), jnp.int32),
            V((4, 4, 3, 1, TOKENS), f32),
            V((4, 4, 8, 128), f32),
            V((2, VOCAB, 512), bf16),
            pltpu.SemaphoreType.DMA((N_SEMS,)),
            pltpu.SemaphoreType.DMA((N_SEMS,)),
            pltpu.SemaphoreType.DMA((4,)),
        ],
        compiler_params=pltpu.CompilerParams(
            collective_id=0, has_side_effects=True, vmem_limit_bytes=64 * 1024 * 1024 - 65536
        ),
    )(hidden, weight.T, weight.T, targets.reshape(1, ROWS), mask.reshape(1, ROWS), loss_scale.reshape(1, 1))
    grad_weight = (raw.astype(f32) * clip[0, 0]).astype(bf16).T
    return loss[0, 0], grad_hidden, grad_weight


def solution(mesh):
    torus = Mesh(
        mesh.devices.reshape(4, 4, 2, mesh.shape["tensor"]),
        ("context_0", "context_1", "context_2", "tensor"),
    )
    placed = (P(CONTEXT, "tensor"), P(None, CONTEXT_TENSOR), P(CONTEXT), P(CONTEXT), P())
    return jax.shard_map(
        step,
        mesh=torus,
        in_specs=placed,
        out_specs=(P(), P(CONTEXT, "tensor"), P(None, CONTEXT_TENSOR)),
        check_vma=False,
    )
```

```python
import jax
import jax.numpy as jnp
from jax import lax
from jax.experimental import pallas as pl
from jax.experimental.pallas import tpu as pltpu
from jax.sharding import Mesh
from jax.sharding import PartitionSpec as P

CONTEXT = ("context_0", "context_1", "context_2")
CONTEXT_TENSOR = ("context_0", "context_1", "context_2", "tensor")
MESH_ID = pl.DeviceIdType.MESH

AXIS = {"x": "tensor", "y": "context_1", "z": "context_0", "c": "context_2"}
PARTS = ((0, 384, "xyz"), (384, 384, "yzx"), (768, 256, "zxy"))
ROWS = 32
WIDE = 1024
VOCAB = 1002
EDGE = 1000
PAD = 1024
TOKENS = 1024
ALL = slice(None)
LO, HI, BOTH = pl.ds(0, 16), pl.ds(16, 16), pl.ds(0, 32)
EARLY, N_SEMS = 80, 99

clip_limit = 1.0


def kernel(
    hidden_ref, weight_ref, edge_ref, targets_ref, mask_ref, scale_ref,
    two_ref, gh_ref, raw_ref,
    hid, wgt, soft, dlt, dl, give, take, own, t3, r3, r2, r1, tm, st, plane, final, ended,
    send_sem, recv_sem, local_sem,
):
    f32, bf16 = jnp.float32, jnp.bfloat16
    me = {k: lax.axis_index(a) for k, a in AXIS.items()}
    up = {k: lax.rem(me[k] + 1, 4) for k in "xyz"}
    down = {k: lax.rem(me[k] + 3, 4) for k in "xyz"}
    far = {k: lax.rem(me[k] + 2, 4) for k in "xyz"}
    core, sib = me["c"], 1 - me["c"]
    used, sent = [0, EARLY], []

    def device(dim, to):
        return dict(zip((AXIS[d] for d in dim), to if len(dim) > 1 else (to,)))

    def copy(src, dst, dim, to, pool=0):
        k = used[pool]
        used[pool] += 1
        assert k < (EARLY, N_SEMS)[pool]
        c = pltpu.make_async_remote_copy(
            src_ref=src, dst_ref=dst, send_sem=send_sem.at[k], recv_sem=recv_sem.at[k],
            device_id=device(dim, to), device_id_type=MESH_ID,
        )
        c.start()
        sent.append(c)
        return c

    load_w = pltpu.make_async_copy(
        weight_ref.at[pl.ds(0, EDGE)], wgt.at[pl.ds(0, EDGE)], local_sem.at[0]
    )
    load_w.start()
    mine = pltpu.make_async_copy(
        hidden_ref, hid.at[me["x"], core, me["z"], me["y"]], local_sem.at[1]
    )
    mine.start()
    own_tm = tm.at[core, me["z"], me["y"]]
    own_tm[...] = jnp.zeros((8, 128), jnp.int32)
    own_tm[0:1, 0:ROWS] = targets_ref[...]
    own_tm[1:2, 0:ROWS] = mask_ref[...]

    keep = lax.broadcasted_iota(jnp.int32, (8, 4 * WIDE), 0) < VOCAB - EDGE
    edge = jnp.where(keep, edge_ref[...].astype(f32), 0.0)
    rest = jnp.zeros((PAD - EDGE - 8, 4 * WIDE), f32)
    wgt[EDGE:PAD, :] = jnp.concatenate([edge, rest], axis=0).astype(bf16)

    barrier = pltpu.get_barrier_semaphore()
    peers = [(d, where[d]) for d in "xyz" for where in (up, down, far)] + [("c", sib)]
    plane_peers = [("yz", (lax.rem(me["y"] + i, 4), lax.rem(me["z"] + j, 4))) for i in range(4) for j in range(4)]
    plane_peers = plane_peers[1:]
    peers += [plane_peers[4 * i + j - 1] for i in (1, 2, 3) for j in (1, 2, 3)]
    for dim, to in peers:
        pl.semaphore_signal(barrier, inc=1, device_id=device(dim, to), device_id_type=MESH_ID)
    pl.semaphore_wait(barrier, len(peers))
    mine.wait()

    def hview(part, s, v, rows):
        off, w, order = PARTS[part]
        at = {d: (ALL if i < s else (v if i == s else me[d])) for i, d in enumerate(order)}
        return hid.at[at["x"], core, at["z"], at["y"], rows, pl.ds(off, w)]

    def swap(dim, views, to):
        return copy(views, views, dim, to)

    def gather_start(part, s):
        d = PARTS[part][2][s]
        lo, hi = hview(part, s, me[d], LO), hview(part, s, me[d], HI)
        a = swap(d, lo, up[d])
        b = swap(d, hi, down[d])
        e = swap(d, hi, up[d])
        f = swap(d, lo, down[d])
        return a, b, e, f

    def gather_pass(part, s, cs):
        d = PARTS[part][2][s]
        cs[0].wait_recv()
        g = swap(d, hview(part, s, down[d], LO), up[d])
        cs[1].wait_recv()
        h = swap(d, hview(part, s, up[d], HI), down[d])
        return g, h

    def forward(part, s, v):
        return swap("c", hview(part, s, v, BOTH), sib)

    three = (0, 1, 2)
    ring = (up, down, far)

    def gather_direct(part, s):
        d = PARTS[part][2][s]
        view = hview(part, s, me[d], BOTH)
        return [swap(d, view, to[d]) for to in ring]

    def settle(cs):
        for c in cs:
            c.wait_recv()

    tcs = [copy(own_tm, own_tm, "c", sib)]
    for s in (0, 1):
        started = [gather_direct(p, s) for p in three]
        settle(tcs)
        view = tm.at[:, me["z"], me["y"]] if s == 0 else tm.at[:, me["z"]]
        tcs = [copy(view, view, "yz"[s], to["yz"[s]]) for to in ring]
        for p in three:
            settle(started[p])

    fwd = [forward(p, 2, me[PARTS[p][2][2]]) for p in three]
    started = [gather_start(p, 2) for p in three]
    passed = [gather_pass(p, 2, started[p]) for p in three]
    for p in (2, 0, 1):
        d = PARTS[p][2][2]
        started[p][2].wait_recv()
        fwd.append(forward(p, 2, down[d]))
        started[p][3].wait_recv()
        fwd.append(forward(p, 2, up[d]))
    for p in (2, 0, 1):
        settle(passed[p])
        fwd.append(forward(p, 2, far[PARTS[p][2][2]]))
    load_w.wait()
    settle(tcs)

    def logits_of(c):
        @pl.loop(0, 2)
        def _(n):
            cols = pl.ds(pl.multiple_of(c * 512 + n * 256, 256), 256)
            for x in range(4):
                rows = hid[x, c, pl.ds(2 * n, 2)].reshape(256, WIDE)
                part = lax.dot_general(
                    wgt[:, x * WIDE : (x + 1) * WIDE], rows, (((1,), (1,)), ((), ())),
                    preferred_element_type=f32,
                )
                if x == 0:
                    soft[:, cols] = part
                else:
                    soft[:, cols] += part

    logits_of(core)
    settle(fwd)
    logits_of(sib)
    for c in sent:
        c.wait_send()
    sent.clear()
    used[0] = 0

    def by_token(row):
        groups = []
        for c in range(2):
            for z in range(4):
                total = tm[c, z, 0, row : row + 1, :]
                for y in range(1, 4):
                    total = total + pltpu.roll(tm[c, z, y, row : row + 1, :], ROWS * y, 1)
                groups.append(total)
        return jnp.concatenate(groups, axis=1)

    targets = by_token(0)
    maskf = by_token(1).astype(f32)

    place = ((me["z"] * 4 + me["y"]) * 2 + core) * 4 + me["x"]
    first = place * VOCAB
    vocab_row = lax.broadcasted_iota(jnp.int32, (PAD, 128), 0)
    real = vocab_row < VOCAB
    for n in range(8):
        cols = slice(n * 128, (n + 1) * 128)
        logits = jnp.where(real, soft[:, cols], -jnp.inf)
        top = jnp.max(logits, axis=0, keepdims=True)
        e = jnp.exp(logits - top)
        soft[:, cols] = e
        hit = (vocab_row == targets[:, cols] - first) & real
        st[0, core, 0, :, cols] = top
        st[0, core, 1, :, cols] = jnp.sum(e, axis=0, keepdims=True)
        final[0, core, 0:1, cols] = jnp.sum(jnp.where(hit, logits, 0.0), axis=0, keepdims=True)
    local_top = st[0, core, 0]

    def others(d):
        return (("c", sib),) if d == "c" else tuple((d, w[d]) for w in ring)

    def joined(slots):
        tops = [slot[0] for slot in slots]
        top = tops[0]
        for t in tops[1:]:
            top = jnp.maximum(top, t)
        total = sum(slot[1] * jnp.exp(t - top) for slot, t in zip(slots, tops))
        return top, total

    for i, d in enumerate("cx"):
        view = st.at[i, me[d]]
        settle([copy(view, view, dim, to, 1) for dim, to in others(d)])
        top, total = joined([st.at[i, k] for k in range(2 if d == "c" else 4)])
        nxt = st.at[1, me["x"]] if i == 0 else plane.at[me["y"], me["z"]]
        nxt[0] = top
        nxt[1] = total
    view = plane.at[me["y"], me["z"]]
    settle([copy(view, view, dim, to, 1) for dim, to in plane_peers])
    top, total = joined([plane.at[y, z] for y in range(4) for z in range(4)])

    loss_scale = scale_ref[0, 0]
    denom = jnp.maximum(jnp.sum(maskf, keepdims=True), 1.0)
    factor = loss_scale * maskf / denom
    ratio = jnp.exp(local_top - top) / total

    for n in range(8):
        cols = slice(n * 128, (n + 1) * 128)
        hit = (vocab_row == targets[:, cols] - first) & real
        g = factor[:, cols] * (soft[:, cols] * ratio[:, cols] - jnp.where(hit, 1.0, 0.0))
        g = jnp.where(real, g, 0.0)
        dlt[:, cols] = g.astype(bf16)
        dl[cols, :] = jnp.transpose(g).astype(bf16)

    theirs = pl.ds(pl.multiple_of(sib * 512, 512), 512)
    ours = pl.ds(pl.multiple_of(core * 512, 512), 512)

    def grad_block(x, q):
        cols = pl.ds(pl.multiple_of(x * WIDE + q * 256, 256), 256)
        raw_ref[:, cols] = jnp.dot(dl[...], wgt[:, cols], preferred_element_type=f32)
        at = pl.ds(pl.multiple_of(q * 256, 256), 256)
        give[x, :, :, :, at] = raw_ref[theirs, cols].reshape(4, 4, ROWS, 256).astype(bf16)

    def to_sibling(x, n, off, w):
        at = (pl.ds(x, n), ALL, ALL, ALL, pl.ds(off, w))
        return copy(give.at[at], take.at[at], "c", sib)

    def with_sibling(x, off, w):
        cols = pl.ds(pl.multiple_of(x * WIDE + off, 256), w)
        r = raw_ref[ours, cols].reshape(4, 4, ROWS, w)
        own[x, :, :, :, off : off + w] = (r + take[x, :, :, :, off : off + w].astype(f32)).astype(bf16)

    def gview(part, s, v, rows):
        off, w, order = PARTS[part]
        at = {d: (ALL if i < s else (v if i == s else me[d])) for i, d in enumerate(order)}
        return own.at[at["x"], at["z"], at["y"], rows, pl.ds(off, w)]

    def landing(bufs, k, part, s, rows):
        off, w, _ = PARTS[part]
        lead = (ALL,) * s
        return bufs.at[(k, *lead, rows, pl.ds(off, w))]

    first16 = pl.ds(0, 16)

    def big(part, v, rows, lead):
        off, w, order = PARTS[part]
        at = {order[0]: lead, order[1]: ALL, order[2]: v}
        return own.at[at["x"], at["z"], at["y"], rows, pl.ds(off, w)]

    def big_landing(buf, k, part, rows, lead):
        off, w, _ = PARTS[part]
        return buf.at[k, lead, :, rows, pl.ds(off, w)]

    def scatter_far(part, lead=ALL):
        d = PARTS[part][2][2]
        return [
            copy(big(part, far[d], rows, lead), big_landing(t3, k, part, first16, lead), d, to[d])
            for k, (to, rows) in enumerate(((up, LO), (down, HI)))
        ]

    def scatter_near(part, k, lead=ALL):
        d = PARTS[part][2][2]
        to, rows = ((up, HI), (down, LO))[k]
        return copy(big(part, to[d], rows, lead), big_landing(r3, k, part, rows, lead), d, to[d])

    def scatter_start(part, lead=ALL):
        return scatter_far(part, lead), [scatter_near(part, k, lead) for k in (0, 1)]

    def scatter_pass(part, cs, lead=ALL):
        d = PARTS[part][2][2]
        found = []
        for k, (to, rows) in enumerate(((up, LO), (down, HI))):
            cs[k].wait_recv()
            v = big(part, to[d], rows, lead)
            more = big_landing(t3, k, part, first16, lead)[...]
            v[...] = (v[...].astype(f32) + more.astype(f32)).astype(bf16)
            found.append(copy(v, big_landing(r3, k, part, rows, lead), d, to[d]))
        return found

    def landed(buf, n, part, s):
        total = gview(part, s, me[PARTS[part][2][s]], BOTH)[...].astype(f32)
        for k in range(n):
            total = total + landing(buf, k, part, s, BOTH)[...].astype(f32)
        return total

    def scatter_end(part, cs):
        settle(cs)
        gview(part, 2, me[PARTS[part][2][2]], BOTH)[...] = landed(r3, 2, part, 2).astype(bf16)

    def scatter_direct(part, s):
        d = PARTS[part][2][s]
        buf = r2 if s == 1 else r1
        return [
            copy(gview(part, s, to[d], BOTH), landing(buf, k, part, s, BOTH), d, to[d])
            for k, to in enumerate(ring)
        ]

    raw_sum = final.at[0, core, 1:2, 0:128]

    def weight_grad(first_step, steps):
        @pl.loop(first_step, first_step + steps)
        def _(n):
            x, h = lax.rem(me["x"] + 6 - n // 2, 4), lax.rem(n, 2)
            cols = pl.ds(pl.multiple_of(h * 512, 512), 512)
            at = pl.ds(pl.multiple_of(x * WIDE + h * 512, 512), 512)
            rows = hid[x, :, :, :, :, cols].reshape(TOKENS, 512)
            r = jnp.dot(dlt[...], rows, preferred_element_type=f32)
            raw_ref[:, at] = r
            sq = jnp.sum(r * r, axis=0, keepdims=True)
            raw_sum[...] += sq[:, :128] + sq[:, 128:256] + sq[:, 256:384] + sq[:, 384:]

    final[0, core, 1:2, :] = jnp.zeros((1, TOKENS), f32)
    def last_columns(first_x):
        @pl.loop(first_x, first_x + 2)
        def _(x):
            grad_block(x, 3)

        return to_sibling(first_x, 2, 768, 256)

    x_order = [w["x"] for w in (far, up, down, me)]
    rest = [last_columns(0), last_columns(2)]
    pair, far_a, near_a, near_b = [], [], [], []

    def finish(i):
        settle([pair[i]])
        with_sibling(x_order[i], 0, 768)
        a, b = scatter_start(0, x_order[i])
        far_a.append(a)
        near_a.extend(b)
        if i == 0:
            near_b.append(scatter_far(1))
        elif i < 3:
            near_b.append(scatter_near(1, i - 1))

    for i in range(4):
        @pl.loop(0, 3)
        def _(q):
            grad_block(x_order[i], q)

        pair.append(to_sibling(x_order[i], 1, 0, 768))
        if i == 0:
            settle(rest)
            for x in range(4):
                with_sibling(x, 768, 256)
            far_c, near_c = scatter_start(2)
        else:
            finish(i - 1)
    weight_grad(0, 1)
    finish(3)
    pass_c = scatter_pass(2, far_c)
    pass_a = scatter_pass(0, far_a[0], x_order[0])
    pass_b = scatter_pass(1, near_b[0])
    weight_grad(1, 1)
    pass_a += scatter_pass(0, far_a[1], x_order[1])
    weight_grad(2, 2)
    pass_a += scatter_pass(0, far_a[2], x_order[2])
    pass_a += scatter_pass(0, far_a[3], x_order[3])
    weight_grad(4, 4)
    big_ends = ([*near_a, *pass_a], [*near_b[1:], *pass_b], [*near_c, *pass_c])

    view = final.at[0, core]
    settle([copy(view, view, "c", sib)])
    final[1, me["x"]] = final[0, 0] + final[0, 1]
    view = final.at[1, me["x"]]
    q = [copy(view, view, "x", to["x"]) for to in ring]
    cs2, cs1 = [None] * 3, [None] * 3
    for p in (2, 1, 0):
        scatter_end(p, big_ends[p])
        cs2[p] = scatter_direct(p, 1)
    settle(q)
    ended[me["y"], me["z"]] = sum(final[1, k] for k in range(4))
    view = ended.at[me["y"], me["z"]]
    q = [copy(view, view, dim, to) for dim, to in plane_peers]
    for p in (2, 1, 0):
        settle(cs2[p])
        v = gview(p, 1, me[PARTS[p][2][1]], BOTH)
        v[...] = landed(r2, 3, p, 1).astype(bf16)
        cs1[p] = scatter_direct(p, 0)
    for p in (2, 1, 0):
        settle(cs1[p])
        off, w, _ = PARTS[p]
        gh_ref[:, off : off + w] = landed(r1, 3, p, 0).astype(bf16)
    settle(q)
    ending = sum(ended[y, z] for y in range(4) for z in range(4))
    token_loss = jnp.log(total) + top - ending[0:1]
    loss = jnp.sum(maskf * token_loss, keepdims=True) / denom
    squares = jnp.sum(ending[1:2, 0:128], keepdims=True)
    norm = jnp.sqrt(squares) / loss_scale
    clip = clip_limit / jnp.maximum(norm, clip_limit)
    two_ref[0:1, :] = jnp.broadcast_to(loss, (1, 128))
    two_ref[1:2, :] = jnp.broadcast_to(clip, (1, 128))
    for c in sent:
        c.wait_send()


def scaled(two_ref, gh_in, raw_ref, loss_ref, gh_out, out_ref, buf, sems):
    near = pltpu.make_async_copy(gh_in, gh_out, sems.at[8])
    near.start()
    clip = two_ref[1:2, 0:1]
    loss_ref[...] = two_ref[0:1, 0:1]
    copies = []
    for n in range(8):
        cols = slice(n * 512, (n + 1) * 512)
        buf[n] = (raw_ref[0:VOCAB, cols] * clip).astype(jnp.bfloat16)
        c = pltpu.make_async_copy(buf.at[n], out_ref.at[:, cols], sems.at[n])
        c.start()
        copies.append(c)
    near.wait()
    for c in copies:
        c.wait()


def step(hidden, weight, targets, mask, loss_scale):
    f32, bf16 = jnp.float32, jnp.bfloat16
    any_space = pl.BlockSpec(memory_space=pl.ANY)
    vmem = pl.BlockSpec(memory_space=pltpu.VMEM)
    smem = pl.BlockSpec(memory_space=pltpu.SMEM)
    V = pltpu.VMEM
    two, near, raw = pl.pallas_call(
        kernel,
        out_shape=(V((8, 128), f32), V((ROWS, WIDE), bf16), V((PAD, 4 * WIDE), f32)),
        grid=(1,),
        in_specs=[
            any_space, any_space, pl.BlockSpec((8, 4 * WIDE), lambda i: (EDGE // 8, 0)), vmem, vmem, smem,
        ],
        out_specs=(vmem, vmem, vmem),
        scratch_shapes=[
            V((4, 2, 4, 4, ROWS, WIDE), bf16),
            V((PAD, 4 * WIDE), bf16),
            V((PAD, TOKENS), f32),
            V((PAD, TOKENS), bf16),
            V((TOKENS, PAD), bf16),
            V((4, 4, 4, ROWS, WIDE), bf16),
            V((4, 4, 4, ROWS, WIDE), bf16),
            V((4, 4, 4, ROWS, WIDE), bf16),
            V((2, 4, 4, 16, WIDE), bf16),
            V((2, 4, 4, ROWS, WIDE), bf16),
            V((3, 4, ROWS, WIDE), bf16),
            V((3, ROWS, WIDE), bf16),
            V((2, 4, 4, 8, 128), jnp.int32),
            V((2, 4, 2, 1, TOKENS), f32),
            V((4, 4, 2, 1, TOKENS), f32),
            V((2, 4, 2, TOKENS), f32),
            V((4, 4, 2, TOKENS), f32),
            pltpu.SemaphoreType.DMA((N_SEMS,)),
            pltpu.SemaphoreType.DMA((N_SEMS,)),
            pltpu.SemaphoreType.DMA((4,)),
        ],
        compiler_params=pltpu.CompilerParams(
            collective_id=0, has_side_effects=True, vmem_limit_bytes=95 * 512 * 1024
        ),
    )(hidden, weight.T, weight.T, targets.reshape(1, ROWS), mask.reshape(1, ROWS), loss_scale.reshape(1, 1))
    loss, grad_hidden, grad_weight = pl.pallas_call(
        scaled,
        out_shape=(
            jax.ShapeDtypeStruct((1, 1), f32),
            jax.ShapeDtypeStruct((ROWS, WIDE), bf16),
            jax.ShapeDtypeStruct((VOCAB, 4 * WIDE), bf16),
        ),
        in_specs=[vmem, vmem, vmem],
        out_specs=(vmem, any_space, any_space),
        scratch_shapes=[V((8, VOCAB, 512), bf16), pltpu.SemaphoreType.DMA((9,))],
        compiler_params=pltpu.CompilerParams(vmem_limit_bytes=24 * 1024 * 1024),
    )(two, near, raw)
    return loss[0, 0], grad_hidden, grad_weight.T


def solution(mesh):
    torus = Mesh(
        mesh.devices.reshape(4, 4, 2, mesh.shape["tensor"]),
        ("context_0", "context_1", "context_2", "tensor"),
    )
    placed = (P(CONTEXT, "tensor"), P(None, CONTEXT_TENSOR), P(CONTEXT), P(CONTEXT), P())
    return jax.shard_map(
        step,
        mesh=torus,
        in_specs=placed,
        out_specs=(P(), P(CONTEXT, "tensor"), P(None, CONTEXT_TENSOR)),
        check_vma=False,
    )
```

```python
import jax
import jax.numpy as jnp
from jax import lax
from jax.experimental import pallas as pl
from jax.experimental.pallas import tpu as pltpu
from jax.sharding import Mesh
from jax.sharding import PartitionSpec as P

CONTEXT = ("context_0", "context_1", "context_2")
CONTEXT_TENSOR = ("context_0", "context_1", "context_2", "tensor")
MESH_ID = pl.DeviceIdType.MESH

AXIS = {"x": "tensor", "y": "context_1", "z": "context_0", "c": "context_2"}
PARTS = ((0, 384, "xyz"), (384, 384, "yzx"), (768, 256, "zxy"))
ROWS = 32
WIDE = 1024
VOCAB = 1002
EDGE = 1000
PAD = 1024
TOKENS = 1024
ALL = slice(None)
LO, HI, BOTH = pl.ds(0, 16), pl.ds(16, 16), pl.ds(0, 32)
EARLY, N_SEMS = 103, 125

clip_limit = 1.0


def kernel(
    hidden_ref, weight_ref, edge_ref, targets_ref, mask_ref, scale_ref,
    two_ref, gh_ref, raw_ref,
    hid, wgt, soft, dlt, dl, give, take, own, t3, r3, r2, r1, tm, st, plane, final, ended,
    send_sem, recv_sem, local_sem,
):
    f32, bf16 = jnp.float32, jnp.bfloat16
    me = {k: lax.axis_index(a) for k, a in AXIS.items()}
    up = {k: lax.rem(me[k] + 1, 4) for k in "xyz"}
    down = {k: lax.rem(me[k] + 3, 4) for k in "xyz"}
    far = {k: lax.rem(me[k] + 2, 4) for k in "xyz"}
    core, sib = me["c"], 1 - me["c"]
    used, sent = [0, EARLY], []

    def device(dim, to):
        return dict(zip((AXIS[d] for d in dim), to if len(dim) > 1 else (to,)))

    def copy(src, dst, dim, to, pool=0):
        k = used[pool]
        used[pool] += 1
        assert k < (EARLY, N_SEMS)[pool]
        c = pltpu.make_async_remote_copy(
            src_ref=src, dst_ref=dst, send_sem=send_sem.at[k], recv_sem=recv_sem.at[k],
            device_id=device(dim, to), device_id_type=MESH_ID,
        )
        c.start()
        sent.append(c)
        return c

    load_w = pltpu.make_async_copy(
        weight_ref.at[pl.ds(0, EDGE)], wgt.at[pl.ds(0, EDGE)], local_sem.at[0]
    )
    load_w.start()
    mine = [
        pltpu.make_async_copy(
            hidden_ref.at[pl.ds(16 * h, 16)], hid.at[h, me["x"], core, me["z"], me["y"]],
            local_sem.at[1 + h],
        )
        for h in range(2)
    ]
    for c in mine:
        c.start()
    own_tm = tm.at[core, me["z"], me["y"]]
    own_tm[...] = jnp.zeros((8, 128), jnp.int32)
    for h in range(2):
        own_tm[h : h + 1, 0:16] = targets_ref[:, 16 * h : 16 * h + 16]
        own_tm[2 + h : 3 + h, 0:16] = mask_ref[:, 16 * h : 16 * h + 16]

    keep = lax.broadcasted_iota(jnp.int32, (8, 4 * WIDE), 0) < VOCAB - EDGE
    edge = jnp.where(keep, edge_ref[...].astype(f32), 0.0)
    rest = jnp.zeros((PAD - EDGE - 8, 4 * WIDE), f32)
    wgt[EDGE:PAD, :] = jnp.concatenate([edge, rest], axis=0).astype(bf16)

    barrier = pltpu.get_barrier_semaphore()
    peers = [(d, where[d]) for d in "xyz" for where in (up, down, far)] + [("c", sib)]
    plane_peers = [("yz", (lax.rem(me["y"] + i, 4), lax.rem(me["z"] + j, 4))) for i in range(4) for j in range(4)]
    plane_peers = plane_peers[1:]
    line_peers = [("xc", (lax.rem(me["x"] + i, 4), c)) for i in range(4) for c in (core, sib)][1:]
    peers += [p for k, p in enumerate(line_peers) if k in (2, 4, 6)]
    peers += [plane_peers[4 * i + j - 1] for i in (1, 2, 3) for j in (1, 2, 3)]
    for dim, to in peers:
        pl.semaphore_signal(barrier, inc=1, device_id=device(dim, to), device_id_type=MESH_ID)
    pl.semaphore_wait(barrier, len(peers))
    for c in mine:
        c.wait()

    def hview(part, s, v, h, rows=ALL):
        off, w, order = PARTS[part]
        at = {d: (ALL if i < s else (v if i == s else me[d])) for i, d in enumerate(order)}
        return hid.at[h, at["x"], core, at["z"], at["y"], rows, pl.ds(off, w)]

    def eighth(k):
        return pl.ds(8 * k, 8)

    def gather_start(part, h):
        d = PARTS[part][2][2]
        lo, hi = (hview(part, 2, me[d], h, eighth(k)) for k in range(2))
        a = swap(d, lo, up[d])
        b = swap(d, hi, down[d])
        e = swap(d, hi, up[d])
        f = swap(d, lo, down[d])
        return a, b, e, f

    def gather_pass(part, h, cs):
        d = PARTS[part][2][2]
        cs[0].wait_recv()
        g = swap(d, hview(part, 2, down[d], h, eighth(0)), up[d])
        cs[1].wait_recv()
        return g, swap(d, hview(part, 2, up[d], h, eighth(1)), down[d])

    def swap(dim, view, to):
        return copy(view, view, dim, to)

    def forward(part, v, h):
        return swap("c", hview(part, 2, v, h), sib)

    three = (0, 1, 2)
    ring = (up, down, far)

    def gather_direct(part, s, h):
        d = PARTS[part][2][s]
        view = hview(part, s, me[d], h)
        return [swap(d, view, to[d]) for to in ring]

    def settle(cs):
        for c in cs:
            c.wait_recv()

    def hop(s, h):
        return [c for p in three for c in gather_direct(p, s, h)]

    def bulk(h):
        near = [forward(p, me[PARTS[p][2][2]], h) for p in three]
        return near, [gather_start(p, h) for p in three]

    def arrived(h, fwd, started, passed):
        for p in (2, 0, 1):
            d = PARTS[p][2][2]
            started[p][2].wait_recv()
            fwd.append(forward(p, down[d], h))
            started[p][3].wait_recv()
            fwd.append(forward(p, up[d], h))
        for p in (2, 0, 1):
            settle(passed[p])
            fwd.append(forward(p, far[PARTS[p][2][2]], h))

    once = jnp.minimum(me["x"] + 1, 1)

    def logits_of(c, h):
        @pl.loop(0, once)
        def _(n):
            cols = pl.ds(pl.multiple_of(h * 512 + c * 256 + n * 256, 256), 256)
            for x in range(4):
                rows = hid[h, x, c].reshape(256, WIDE)
                part = lax.dot_general(
                    wgt[:, x * WIDE : (x + 1) * WIDE], rows, (((1,), (1,)), ((), ())),
                    preferred_element_type=f32,
                )
                if x == 0:
                    soft[:, cols] = part
                else:
                    soft[:, cols] += part

    tcs = [copy(own_tm, own_tm, "c", sib)]
    hops = [hop(0, h) for h in (0, 1)]
    settle(hops[0])
    first = hop(1, 0)
    settle(tcs)
    view = tm.at[:, me["z"], me["y"]]
    tcs = [copy(view, view, "y", to["y"]) for to in ring]
    settle(hops[1])
    second = hop(1, 1)
    settle(first)
    fwd0, started0 = bulk(0)
    settle(second)
    settle(tcs)
    view = tm.at[:, me["z"]]
    tcs = [copy(view, view, "z", to["z"]) for to in ring]
    passed0 = [gather_pass(p, 0, started0[p]) for p in three]
    fwd1, started1 = bulk(1)
    arrived(0, fwd0, started0, passed0)
    load_w.wait()
    logits_of(core, 0)
    passed1 = [gather_pass(p, 1, started1[p]) for p in three]
    settle(fwd0)
    logits_of(sib, 0)
    arrived(1, fwd1, started1, passed1)
    logits_of(core, 1)
    settle(fwd1)
    settle(tcs)
    logits_of(sib, 1)
    for c in sent:
        c.wait_send()
    sent.clear()
    used[0] = 0

    def by_token(row):
        groups = []
        for h in range(2):
            for c in range(2):
                for pair in range(2):
                    total = jnp.zeros((1, 128), jnp.int32)
                    for k in range(8):
                        piece = tm[c, 2 * pair + k // 4, k % 4, row + h : row + h + 1, :]
                        total = total + (pltpu.roll(piece, 16 * k, 1) if k else piece)
                    groups.append(total)
        return jnp.concatenate(groups, axis=1)

    targets = by_token(0)
    maskf = by_token(2).astype(f32)

    place = ((me["z"] * 4 + me["y"]) * 2 + core) * 4 + me["x"]
    first_id = place * VOCAB
    vocab_row = lax.broadcasted_iota(jnp.int32, (PAD, 128), 0)
    real = vocab_row < VOCAB
    for n in range(8):
        cols = slice(n * 128, (n + 1) * 128)
        logits = jnp.where(real, soft[:, cols], -jnp.inf)
        top = jnp.max(logits, axis=0, keepdims=True)
        e = jnp.exp(logits - top)
        soft[:, cols] = e
        hit = (vocab_row == targets[:, cols] - first_id) & real
        st[core, me["x"], 0, :, cols] = top
        st[core, me["x"], 1, :, cols] = jnp.sum(e, axis=0, keepdims=True)
        final[core, me["x"], 0:1, cols] = jnp.sum(jnp.where(hit, logits, 0.0), axis=0, keepdims=True)
    local_top = st[core, me["x"], 0]

    def joined(slots):
        tops = [slot[0] for slot in slots]
        top = tops[0]
        for t in tops[1:]:
            top = jnp.maximum(top, t)
        total = sum(slot[1] * jnp.exp(t - top) for slot, t in zip(slots, tops))
        return top, total

    eight = [(c, x) for c in range(2) for x in range(4)]
    view = st.at[core, me["x"]]
    settle([copy(view, view, dim, to, 1) for dim, to in line_peers])
    top, total = joined([st.at[c, x] for c, x in eight])
    plane[me["y"], me["z"], 0] = top
    plane[me["y"], me["z"], 1] = total
    view = plane.at[me["y"], me["z"]]
    settle([copy(view, view, dim, to, 1) for dim, to in plane_peers])
    top, total = joined([plane.at[y, z] for y in range(4) for z in range(4)])

    loss_scale = scale_ref[0]
    denom = jnp.maximum(jnp.sum(maskf, keepdims=True), 1.0)
    factor = loss_scale * maskf / denom
    ratio = jnp.exp(local_top - top) / total

    for n in range(8):
        cols = slice(n * 128, (n + 1) * 128)
        hit = (vocab_row == targets[:, cols] - first_id) & real
        g = factor[:, cols] * (soft[:, cols] * ratio[:, cols] - jnp.where(hit, 1.0, 0.0))
        g = jnp.where(real, g, 0.0)
        dlt[:, cols] = g.astype(bf16)
        at = (core if n // 2 % 2 else sib) * 512 + (n // 4 * 2 + n % 2) * 128
        at = pl.multiple_of(at, 128)
        dl[pl.ds(at, 128), :] = jnp.transpose(g).astype(bf16)

    def grad_block(x, q):
        cols = pl.ds(pl.multiple_of(x * WIDE + q * 256, 256), 256)
        r = jnp.dot(dl[...], wgt[:, cols], preferred_element_type=f32)
        raw_ref[512:, cols] = r[512:]
        at = pl.ds(pl.multiple_of(q * 256, 256), 256)
        for h in range(2):
            rows = r[256 * h : 256 * h + 256].reshape(4, 4, 16, 256)
            give[x, :, :, 16 * h : 16 * h + 16, at] = rows.astype(bf16)

    def to_sibling(x, n, off, w):
        at = (pl.ds(x, n), ALL, ALL, ALL, pl.ds(off, w))
        return copy(give.at[at], take.at[at], "c", sib)

    def with_sibling(x, off, w):
        cols = pl.ds(pl.multiple_of(x * WIDE + off, 256), w)
        for h in range(2):
            at = (x, ALL, ALL, slice(16 * h, 16 * h + 16), slice(off, off + w))
            r = raw_ref[512 + 256 * h : 768 + 256 * h, cols].reshape(4, 4, 16, w)
            own[at] = (r + take[at].astype(f32)).astype(bf16)

    def gview(part, s, v, rows):
        off, w, order = PARTS[part]
        at = {d: (ALL if i < s else (v if i == s else me[d])) for i, d in enumerate(order)}
        return own.at[at["x"], at["z"], at["y"], rows, pl.ds(off, w)]

    def landing(bufs, k, part, s, rows):
        off, w, _ = PARTS[part]
        lead = (ALL,) * s
        return bufs.at[(k, *lead, rows, pl.ds(off, w))]

    first16 = pl.ds(0, 16)

    def big(part, v, rows, lead):
        off, w, order = PARTS[part]
        at = {order[0]: lead, order[1]: ALL, order[2]: v}
        return own.at[at["x"], at["z"], at["y"], rows, pl.ds(off, w)]

    def big_landing(buf, k, part, rows, lead):
        off, w, _ = PARTS[part]
        return buf.at[k, lead, :, rows, pl.ds(off, w)]

    def scatter_far(part, lead=ALL):
        d = PARTS[part][2][2]
        return [
            copy(big(part, far[d], rows, lead), big_landing(t3, k, part, first16, lead), d, to[d])
            for k, (to, rows) in enumerate(((up, LO), (down, HI)))
        ]

    def scatter_near(part, k, lead=ALL):
        d = PARTS[part][2][2]
        to, rows = ((up, HI), (down, LO))[k]
        return copy(big(part, to[d], rows, lead), big_landing(r3, k, part, rows, lead), d, to[d])

    def scatter_start(part, lead=ALL):
        return scatter_far(part, lead), [scatter_near(part, k, lead) for k in (0, 1)]

    def scatter_pass(part, cs, lead=ALL):
        d = PARTS[part][2][2]
        found = []
        for k, (to, rows) in enumerate(((up, LO), (down, HI))):
            cs[k].wait_recv()
            v = big(part, to[d], rows, lead)
            more = big_landing(t3, k, part, first16, lead)[...]
            v[...] = (v[...].astype(f32) + more.astype(f32)).astype(bf16)
            found.append(copy(v, big_landing(r3, k, part, rows, lead), d, to[d]))
        return found

    def landed(buf, n, part, s):
        total = gview(part, s, me[PARTS[part][2][s]], BOTH)[...].astype(f32)
        for k in range(n):
            total = total + landing(buf, k, part, s, BOTH)[...].astype(f32)
        return total

    def scatter_end(part, cs):
        settle(cs)
        gview(part, 2, me[PARTS[part][2][2]], BOTH)[...] = landed(r3, 2, part, 2).astype(bf16)

    def scatter_direct(part, s):
        d = PARTS[part][2][s]
        buf = r2 if s == 1 else r1
        return [
            copy(gview(part, s, to[d], BOTH), landing(buf, k, part, s, BOTH), d, to[d])
            for k, to in enumerate(ring)
        ]

    raw_sum = final.at[core, me["x"], 1:2, 0:128]

    def weight_grad(first_step, steps):
        @pl.loop(first_step, first_step + steps)
        def _(n):
            x, h = lax.rem(me["x"] + 6 - n // 2, 4), lax.rem(n, 2)
            cols = pl.ds(pl.multiple_of(h * 512, 512), 512)
            at = pl.ds(pl.multiple_of(x * WIDE + h * 512, 512), 512)
            r = None
            for half in range(2):
                rows = hid[half, x, :, :, :, :, cols].reshape(512, 512)
                part = jnp.dot(dlt[:, 512 * half : 512 * half + 512], rows, preferred_element_type=f32)
                r = part if r is None else r + part
            raw_ref[:, at] = r
            sq = jnp.sum(r * r, axis=0, keepdims=True)
            raw_sum[...] += sq[:, :128] + sq[:, 128:256] + sq[:, 256:384] + sq[:, 384:]

    final[core, me["x"], 1:2, :] = jnp.zeros((1, TOKENS), f32)
    def last_columns(first_x):
        @pl.loop(first_x, first_x + 2)
        def _(x):
            grad_block(x, 3)

        return to_sibling(first_x, 2, 768, 256)

    x_order = [w["x"] for w in (far, up, down, me)]
    rest = [last_columns(0), last_columns(2)]
    pair, far_a, near_a, near_b = [], [], [], []

    def finish(i):
        settle([pair[i]])
        with_sibling(x_order[i], 0, 768)
        a, b = scatter_start(0, x_order[i])
        far_a.append(a)
        near_a.extend(b)
        if i == 0:
            near_b.append(scatter_far(1))
        elif i < 3:
            near_b.append(scatter_near(1, i - 1))

    for i in range(4):
        @pl.loop(0, 3)
        def _(q):
            grad_block(x_order[i], q)

        pair.append(to_sibling(x_order[i], 1, 0, 768))
        if i > 0:
            finish(i - 1)
        if i == 1:
            settle(rest)
            for x in range(4):
                with_sibling(x, 768, 256)
            far_c, near_c = scatter_start(2)
        if i == 3:
            pass_a = scatter_pass(0, far_a[0], x_order[0])
    weight_grad(0, 1)
    pass_b = scatter_pass(1, near_b[0])
    finish(3)
    pass_c = scatter_pass(2, far_c)
    pass_a += scatter_pass(0, far_a[1], x_order[1])
    weight_grad(1, 2)
    pass_a += scatter_pass(0, far_a[2], x_order[2])
    weight_grad(3, 2)
    pass_a += scatter_pass(0, far_a[3], x_order[3])
    weight_grad(5, 1)
    big_ends = ([*near_a, *pass_a], [*near_b[1:], *pass_b], [*near_c, *pass_c])
    cs2, cs1 = [None] * 3, [None] * 3

    def middle(p):
        scatter_end(p, big_ends[p])
        cs2[p] = scatter_direct(p, 1)

    middle(2)
    weight_grad(6, 2)

    view = final.at[core, me["x"]]
    q = [copy(view, view, dim, to) for dim, to in line_peers]
    middle(1)
    middle(0)
    settle(q)
    ended[me["y"], me["z"]] = sum(final[c, x] for c, x in eight)
    view = ended.at[me["y"], me["z"]]
    q = [copy(view, view, dim, to) for dim, to in plane_peers]
    for p in (2, 1, 0):
        settle(cs2[p])
        v = gview(p, 1, me[PARTS[p][2][1]], BOTH)
        v[...] = landed(r2, 3, p, 1).astype(bf16)
        cs1[p] = scatter_direct(p, 0)
    for p in (2, 1, 0):
        settle(cs1[p])
        off, w, _ = PARTS[p]
        gh_ref[:, off : off + w] = landed(r1, 3, p, 0).astype(bf16)
    settle(q)
    ending = sum(ended[y, z] for y in range(4) for z in range(4))
    token_loss = jnp.log(total) + top - ending[0:1]
    loss = jnp.sum(maskf * token_loss, keepdims=True) / denom
    squares = jnp.sum(ending[1:2, 0:128], keepdims=True)
    norm = jnp.sqrt(squares) / loss_scale
    clip = clip_limit / jnp.maximum(norm, clip_limit)
    two_ref[0:1, :] = jnp.broadcast_to(loss, (1, 128))
    two_ref[1:2, :] = jnp.broadcast_to(clip, (1, 128))
    for c in sent:
        c.wait_send()


def scaled(two_ref, gh_in, raw_ref, loss_ref, gh_out, out_ref, buf, sems):
    near = pltpu.make_async_copy(gh_in, gh_out, sems.at[8])
    near.start()
    clip = two_ref[1:2, 0:1]
    loss_ref[...] = two_ref[0:1, 0:1]
    copies = []
    for n in range(8):
        cols = slice(n * 512, (n + 1) * 512)
        buf[n] = (raw_ref[0:VOCAB, cols] * clip).astype(jnp.bfloat16)
        c = pltpu.make_async_copy(buf.at[n], out_ref.at[:, cols], sems.at[n])
        c.start()
        copies.append(c)
    near.wait()
    for c in copies:
        c.wait()


def step(hidden, weight, targets, mask, loss_scale):
    f32, bf16 = jnp.float32, jnp.bfloat16
    any_space = pl.BlockSpec(memory_space=pl.ANY)
    vmem = pl.BlockSpec(memory_space=pltpu.VMEM)
    smem = pl.BlockSpec(memory_space=pltpu.SMEM)
    V = pltpu.VMEM
    two, near, raw = pl.pallas_call(
        kernel,
        out_shape=(V((8, 128), f32), V((ROWS, WIDE), bf16), V((PAD, 4 * WIDE), f32)),
        grid=(1,),
        in_specs=[
            any_space, any_space, pl.BlockSpec((8, 4 * WIDE), lambda i: (EDGE // 8, 0)), vmem, vmem, smem,
        ],
        out_specs=(vmem, vmem, vmem),
        scratch_shapes=[
            V((2, 4, 2, 4, 4, 16, WIDE), bf16),
            V((PAD, 4 * WIDE), bf16),
            V((PAD, TOKENS), f32),
            V((PAD, TOKENS), bf16),
            V((TOKENS, PAD), bf16),
            V((4, 4, 4, ROWS, WIDE), bf16),
            V((4, 4, 4, ROWS, WIDE), bf16),
            V((4, 4, 4, ROWS, WIDE), bf16),
            V((2, 4, 4, 16, WIDE), bf16),
            V((2, 4, 4, ROWS, WIDE), bf16),
            V((3, 4, ROWS, WIDE), bf16),
            V((3, ROWS, WIDE), bf16),
            V((2, 4, 4, 8, 128), jnp.int32),
            V((2, 4, 2, 1, TOKENS), f32),
            V((4, 4, 2, 1, TOKENS), f32),
            V((2, 4, 2, TOKENS), f32),
            V((4, 4, 2, TOKENS), f32),
            pltpu.SemaphoreType.DMA((N_SEMS,)),
            pltpu.SemaphoreType.DMA((N_SEMS,)),
            pltpu.SemaphoreType.DMA((4,)),
        ],
        compiler_params=pltpu.CompilerParams(
            collective_id=0, has_side_effects=True, vmem_limit_bytes=95 * 512 * 1024
        ),
    )(hidden, weight.T, weight.T, targets.reshape(1, ROWS), mask.reshape(1, ROWS), loss_scale.reshape(1))
    loss, grad_hidden, grad_weight = pl.pallas_call(
        scaled,
        out_shape=(
            jax.ShapeDtypeStruct((1, 1), f32),
            jax.ShapeDtypeStruct((ROWS, WIDE), bf16),
            jax.ShapeDtypeStruct((VOCAB, 4 * WIDE), bf16),
        ),
        in_specs=[vmem, vmem, vmem],
        out_specs=(vmem, any_space, any_space),
        scratch_shapes=[V((8, VOCAB, 512), bf16), pltpu.SemaphoreType.DMA((9,))],
        compiler_params=pltpu.CompilerParams(vmem_limit_bytes=24 * 1024 * 1024),
    )(two, near, raw)
    return loss[0, 0], grad_hidden, grad_weight.T


def solution(mesh):
    torus = Mesh(
        mesh.devices.reshape(4, 4, 2, mesh.shape["tensor"]),
        ("context_0", "context_1", "context_2", "tensor"),
    )
    placed = (P(CONTEXT, "tensor"), P(None, CONTEXT_TENSOR), P(CONTEXT), P(CONTEXT), P())
    return jax.shard_map(
        step,
        mesh=torus,
        in_specs=placed,
        out_specs=(P(), P(CONTEXT, "tensor"), P(None, CONTEXT_TENSOR)),
        check_vma=False,
    )
```

```python
import jax
import jax.numpy as jnp
from jax import lax
from jax.experimental import pallas as pl
from jax.experimental.pallas import tpu as pltpu
from jax.sharding import Mesh
from jax.sharding import PartitionSpec as P

CONTEXT = ("context_0", "context_1", "context_2")
CONTEXT_TENSOR = ("context_0", "context_1", "context_2", "tensor")
MESH_ID = pl.DeviceIdType.MESH

AXIS = {"x": "tensor", "y": "context_1", "z": "context_0", "c": "context_2"}
PARTS = ((0, 384, "xyz"), (384, 384, "yzx"), (768, 256, "zxy"))
ROWS = 32
WIDE = 1024
VOCAB = 1002
EDGE = 1000
PAD = 1024
TOKENS = 1024
ALL = slice(None)
LO, HI, BOTH = pl.ds(0, 16), pl.ds(16, 16), pl.ds(0, 32)
EARLY, N_SEMS = 103, 125

clip_limit = 1.0


def kernel(
    hidden_ref, weight_ref, edge_ref, targets_ref, mask_ref, scale_ref,
    two_ref, gh_ref, raw_ref,
    hid, wgt, soft, dlt, dl, give, take, own, t3, r3, r2, r1, tm, st, plane, final, ended,
    send_sem, recv_sem, local_sem,
):
    f32, bf16 = jnp.float32, jnp.bfloat16
    me = {k: lax.axis_index(a) for k, a in AXIS.items()}
    up = {k: lax.rem(me[k] + 1, 4) for k in "xyz"}
    down = {k: lax.rem(me[k] + 3, 4) for k in "xyz"}
    far = {k: lax.rem(me[k] + 2, 4) for k in "xyz"}
    core, sib = me["c"], 1 - me["c"]
    used, sent = [0, EARLY], []

    def device(dim, to):
        return dict(zip((AXIS[d] for d in dim), to if len(dim) > 1 else (to,)))

    def copy(src, dst, dim, to, pool=0):
        k = used[pool]
        used[pool] += 1
        assert k < (EARLY, N_SEMS)[pool]
        c = pltpu.make_async_remote_copy(
            src_ref=src, dst_ref=dst, send_sem=send_sem.at[k], recv_sem=recv_sem.at[k],
            device_id=device(dim, to), device_id_type=MESH_ID,
        )
        c.start()
        sent.append(c)
        return c

    load_w = pltpu.make_async_copy(
        weight_ref.at[pl.ds(0, EDGE)], wgt.at[pl.ds(0, EDGE)], local_sem.at[0]
    )
    load_w.start()
    mine = [
        pltpu.make_async_copy(
            hidden_ref.at[pl.ds(16 * h, 16)], hid.at[h, me["x"], core, me["z"], me["y"]],
            local_sem.at[1 + h],
        )
        for h in range(2)
    ]
    for c in mine:
        c.start()
    own_tm = tm.at[core, me["z"], me["y"]]
    own_tm[...] = jnp.zeros((8, 128), jnp.int32)
    for h in range(2):
        own_tm[h : h + 1, 0:16] = targets_ref[:, 16 * h : 16 * h + 16]
        own_tm[2 + h : 3 + h, 0:16] = mask_ref[:, 16 * h : 16 * h + 16]

    keep = lax.broadcasted_iota(jnp.int32, (8, 4 * WIDE), 0) < VOCAB - EDGE
    edge = jnp.where(keep, edge_ref[...].astype(f32), 0.0)
    rest = jnp.zeros((PAD - EDGE - 8, 4 * WIDE), f32)
    wgt[EDGE:PAD, :] = jnp.concatenate([edge, rest], axis=0).astype(bf16)

    barrier = pltpu.get_barrier_semaphore()
    peers = [(d, where[d]) for d in "xyz" for where in (up, down, far)] + [("c", sib)]
    plane_peers = [("yz", (lax.rem(me["y"] + i, 4), lax.rem(me["z"] + j, 4))) for i in range(4) for j in range(4)]
    plane_peers = plane_peers[1:]
    line_peers = [("xc", (lax.rem(me["x"] + i, 4), c)) for i in range(4) for c in (core, sib)][1:]
    peers += [p for k, p in enumerate(line_peers) if k in (2, 4, 6)]
    peers += [plane_peers[4 * i + j - 1] for i in (1, 2, 3) for j in (1, 2, 3)]
    for dim, to in peers:
        pl.semaphore_signal(barrier, inc=1, device_id=device(dim, to), device_id_type=MESH_ID)
    pl.semaphore_wait(barrier, len(peers))
    for c in mine:
        c.wait()

    def hview(part, s, v, h, rows=ALL):
        off, w, order = PARTS[part]
        at = {d: (ALL if i < s else (v if i == s else me[d])) for i, d in enumerate(order)}
        return hid.at[h, at["x"], core, at["z"], at["y"], rows, pl.ds(off, w)]

    def eighth(k):
        return pl.ds(8 * k, 8)

    def gather_start(part, h):
        d = PARTS[part][2][2]
        lo, hi = (hview(part, 2, me[d], h, eighth(k)) for k in range(2))
        a = swap(d, lo, up[d])
        b = swap(d, hi, down[d])
        e = swap(d, hi, up[d])
        f = swap(d, lo, down[d])
        return a, b, e, f

    def gather_pass(part, h, cs):
        d = PARTS[part][2][2]
        cs[0].wait_recv()
        g = swap(d, hview(part, 2, down[d], h, eighth(0)), up[d])
        cs[1].wait_recv()
        return g, swap(d, hview(part, 2, up[d], h, eighth(1)), down[d])

    def swap(dim, view, to):
        return copy(view, view, dim, to)

    def forward(part, v, h):
        return swap("c", hview(part, 2, v, h), sib)

    three = (0, 1, 2)
    ring = (up, down, far)

    def gather_direct(part, s, h):
        d = PARTS[part][2][s]
        view = hview(part, s, me[d], h)
        return [swap(d, view, to[d]) for to in ring]

    def settle(cs):
        for c in cs:
            c.wait_recv()

    def hop(s, h):
        return [c for p in three for c in gather_direct(p, s, h)]

    def bulk(h):
        near = [forward(p, me[PARTS[p][2][2]], h) for p in three]
        return near, [gather_start(p, h) for p in three]

    def arrived(h, fwd, started, passed):
        for p in (2, 0, 1):
            d = PARTS[p][2][2]
            started[p][2].wait_recv()
            fwd.append(forward(p, down[d], h))
            started[p][3].wait_recv()
            fwd.append(forward(p, up[d], h))
        for p in (2, 0, 1):
            settle(passed[p])
            fwd.append(forward(p, far[PARTS[p][2][2]], h))

    once = jnp.minimum(me["x"] + 1, 1)

    def logits_of(c, h):
        @pl.loop(0, once)
        def _(n):
            cols = pl.ds(pl.multiple_of(h * 512 + c * 256 + n * 256, 256), 256)
            for x in range(4):
                rows = hid[h, x, c].reshape(256, WIDE)
                part = lax.dot_general(
                    wgt[:, x * WIDE : (x + 1) * WIDE], rows, (((1,), (1,)), ((), ())),
                    preferred_element_type=f32,
                )
                if x == 0:
                    soft[:, cols] = part
                else:
                    soft[:, cols] += part

    tcs = [copy(own_tm, own_tm, "c", sib)]
    hops = [hop(0, h) for h in (0, 1)]
    settle(hops[0])
    first = hop(1, 0)
    settle(tcs)
    view = tm.at[:, me["z"], me["y"]]
    tcs = [copy(view, view, "y", to["y"]) for to in ring]
    settle(hops[1])
    second = hop(1, 1)
    settle(first)
    fwd0, started0 = bulk(0)
    settle(second)
    settle(tcs)
    view = tm.at[:, me["z"]]
    tcs = [copy(view, view, "z", to["z"]) for to in ring]
    passed0 = [gather_pass(p, 0, started0[p]) for p in three]
    fwd1, started1 = bulk(1)
    arrived(0, fwd0, started0, passed0)
    load_w.wait()
    logits_of(core, 0)
    passed1 = [gather_pass(p, 1, started1[p]) for p in three]
    settle(fwd0)
    logits_of(sib, 0)
    arrived(1, fwd1, started1, passed1)
    logits_of(core, 1)
    settle(fwd1)
    settle(tcs)
    logits_of(sib, 1)
    for c in sent:
        c.wait_send()
    sent.clear()
    used[0] = 0

    def by_token(row):
        groups = []
        for h in range(2):
            for c in range(2):
                for pair in range(2):
                    total = jnp.zeros((1, 128), jnp.int32)
                    for k in range(8):
                        piece = tm[c, 2 * pair + k // 4, k % 4, row + h : row + h + 1, :]
                        total = total + (pltpu.roll(piece, 16 * k, 1) if k else piece)
                    groups.append(total)
        return jnp.concatenate(groups, axis=1)

    targets = by_token(0)
    maskf = by_token(2).astype(f32)

    place = ((me["z"] * 4 + me["y"]) * 2 + core) * 4 + me["x"]
    first_id = place * VOCAB
    vocab_row = lax.broadcasted_iota(jnp.int32, (PAD, 128), 0)
    real = vocab_row < VOCAB
    for n in range(8):
        cols = slice(n * 128, (n + 1) * 128)
        logits = jnp.where(real, soft[:, cols], -jnp.inf)
        top = jnp.max(logits, axis=0, keepdims=True)
        e = jnp.exp(logits - top)
        soft[:, cols] = e
        hit = (vocab_row == targets[:, cols] - first_id) & real
        st[core, me["x"], 0, :, cols] = top
        st[core, me["x"], 1, :, cols] = jnp.sum(e, axis=0, keepdims=True)
        final[core, me["x"], 0:1, cols] = jnp.sum(jnp.where(hit, logits, 0.0), axis=0, keepdims=True)
    local_top = st[core, me["x"], 0]

    def joined(slots):
        tops = [slot[0] for slot in slots]
        top = tops[0]
        for t in tops[1:]:
            top = jnp.maximum(top, t)
        total = sum(slot[1] * jnp.exp(t - top) for slot, t in zip(slots, tops))
        return top, total

    eight = [(c, x) for c in range(2) for x in range(4)]
    view = st.at[core, me["x"]]
    settle([copy(view, view, dim, to, 1) for dim, to in line_peers])
    top, total = joined([st.at[c, x] for c, x in eight])
    plane[me["y"], me["z"], 0] = top
    plane[me["y"], me["z"], 1] = total
    view = plane.at[me["y"], me["z"]]
    settle([copy(view, view, dim, to, 1) for dim, to in plane_peers])
    top, total = joined([plane.at[y, z] for y in range(4) for z in range(4)])

    loss_scale = scale_ref[0]
    denom = jnp.maximum(jnp.sum(maskf, keepdims=True), 1.0)
    factor = loss_scale * maskf / denom
    ratio = jnp.exp(local_top - top) / total

    for n in range(8):
        cols = slice(n * 128, (n + 1) * 128)
        hit = (vocab_row == targets[:, cols] - first_id) & real
        g = factor[:, cols] * (soft[:, cols] * ratio[:, cols] - jnp.where(hit, 1.0, 0.0))
        g = jnp.where(real, g, 0.0)
        dlt[:, cols] = g.astype(bf16)
        at = (core if n // 2 % 2 else sib) * 512 + (n // 4 * 2 + n % 2) * 128
        at = pl.multiple_of(at, 128)
        dl[pl.ds(at, 128), :] = jnp.transpose(g).astype(bf16)

    def grad_block(x, q):
        cols = pl.ds(pl.multiple_of(x * WIDE + q * 256, 256), 256)
        r = jnp.dot(dl[...], wgt[:, cols], preferred_element_type=f32)
        raw_ref[512:, cols] = r[512:]
        at = pl.ds(pl.multiple_of(q * 256, 256), 256)
        for h in range(2):
            rows = r[256 * h : 256 * h + 256].reshape(4, 4, 16, 256)
            give[x, :, :, 16 * h : 16 * h + 16, at] = rows.astype(bf16)

    def to_sibling(x, n, off, w):
        at = (pl.ds(x, n), ALL, ALL, ALL, pl.ds(off, w))
        return copy(give.at[at], take.at[at], "c", sib)

    def with_sibling(x, off, w):
        cols = pl.ds(pl.multiple_of(x * WIDE + off, 256), w)
        for h in range(2):
            at = (x, ALL, ALL, slice(16 * h, 16 * h + 16), slice(off, off + w))
            r = raw_ref[512 + 256 * h : 768 + 256 * h, cols].reshape(4, 4, 16, w)
            own[at] = (r + take[at].astype(f32)).astype(bf16)

    def gview(part, s, v, rows):
        off, w, order = PARTS[part]
        at = {d: (ALL if i < s else (v if i == s else me[d])) for i, d in enumerate(order)}
        return own.at[at["x"], at["z"], at["y"], rows, pl.ds(off, w)]

    def landing(bufs, k, part, s, rows):
        off, w, _ = PARTS[part]
        lead = (ALL,) * s
        return bufs.at[(k, *lead, rows, pl.ds(off, w))]

    first16 = pl.ds(0, 16)

    def big(part, v, rows, lead):
        off, w, order = PARTS[part]
        at = {order[0]: lead, order[1]: ALL, order[2]: v}
        return own.at[at["x"], at["z"], at["y"], rows, pl.ds(off, w)]

    def big_landing(buf, k, part, rows, lead):
        off, w, _ = PARTS[part]
        return buf.at[k, lead, :, rows, pl.ds(off, w)]

    def scatter_far(part, lead=ALL):
        d = PARTS[part][2][2]
        return [
            copy(big(part, far[d], rows, lead), big_landing(t3, k, part, first16, lead), d, to[d])
            for k, (to, rows) in enumerate(((up, LO), (down, HI)))
        ]

    def scatter_near(part, k, lead=ALL):
        d = PARTS[part][2][2]
        to, rows = ((up, HI), (down, LO))[k]
        return copy(big(part, to[d], rows, lead), big_landing(r3, k, part, rows, lead), d, to[d])

    def scatter_start(part, lead=ALL):
        return scatter_far(part, lead), [scatter_near(part, k, lead) for k in (0, 1)]

    def scatter_pass(part, cs, lead=ALL):
        d = PARTS[part][2][2]
        found = []
        for k, (to, rows) in enumerate(((up, LO), (down, HI))):
            cs[k].wait_recv()
            v = big(part, to[d], rows, lead)
            more = big_landing(t3, k, part, first16, lead)[...]
            v[...] = (v[...].astype(f32) + more.astype(f32)).astype(bf16)
            found.append(copy(v, big_landing(r3, k, part, rows, lead), d, to[d]))
        return found

    def landed(buf, n, part, s):
        total = gview(part, s, me[PARTS[part][2][s]], BOTH)[...].astype(f32)
        for k in range(n):
            total = total + landing(buf, k, part, s, BOTH)[...].astype(f32)
        return total

    def scatter_end(part, cs):
        settle(cs)
        gview(part, 2, me[PARTS[part][2][2]], BOTH)[...] = landed(r3, 2, part, 2).astype(bf16)

    def scatter_direct(part, s):
        d = PARTS[part][2][s]
        buf = r2 if s == 1 else r1
        return [
            copy(gview(part, s, to[d], BOTH), landing(buf, k, part, s, BOTH), d, to[d])
            for k, to in enumerate(ring)
        ]

    raw_sum = final.at[core, me["x"], 1:2, 0:128]

    def weight_grad(first_step, steps):
        @pl.loop(first_step, first_step + steps)
        def _(n):
            x, h = lax.rem(me["x"] + 6 - n // 2, 4), lax.rem(n, 2)
            cols = pl.ds(pl.multiple_of(h * 512, 512), 512)
            at = pl.ds(pl.multiple_of(x * WIDE + h * 512, 512), 512)
            r = None
            for half in range(2):
                rows = hid[half, x, :, :, :, :, cols].reshape(512, 512)
                part = jnp.dot(dlt[:, 512 * half : 512 * half + 512], rows, preferred_element_type=f32)
                r = part if r is None else r + part
            raw_ref[:, at] = r
            sq = jnp.sum(r * r, axis=0, keepdims=True)
            raw_sum[...] += sq[:, :128] + sq[:, 128:256] + sq[:, 256:384] + sq[:, 384:]

    final[core, me["x"], 1:2, :] = jnp.zeros((1, TOKENS), f32)
    def last_columns(first_x):
        @pl.loop(first_x, first_x + 2)
        def _(x):
            grad_block(x, 3)

        return to_sibling(first_x, 2, 768, 256)

    x_order = [w["x"] for w in (far, up, down, me)]
    rest = [last_columns(0), last_columns(2)]
    pair, far_a, near_a, near_b = [], [], [], []

    def finish(i):
        settle([pair[i]])
        with_sibling(x_order[i], 0, 768)
        a, b = scatter_start(0, x_order[i])
        far_a.append(a)
        near_a.extend(b)
        if i == 0:
            near_b.append(scatter_far(1))
        elif i < 3:
            near_b.append(scatter_near(1, i - 1))

    for i in range(4):
        @pl.loop(0, 3)
        def _(q):
            grad_block(x_order[i], q)

        pair.append(to_sibling(x_order[i], 1, 0, 768))
        if i > 0:
            finish(i - 1)
        if i == 1:
            settle(rest)
            for x in range(4):
                with_sibling(x, 768, 256)
            far_c, near_c = scatter_start(2)
        if i == 3:
            pass_a = scatter_pass(0, far_a[0], x_order[0])
    weight_grad(0, 1)
    pass_b = scatter_pass(1, near_b[0])
    finish(3)
    pass_c = scatter_pass(2, far_c)
    pass_a += scatter_pass(0, far_a[1], x_order[1])
    weight_grad(1, 2)
    pass_a += scatter_pass(0, far_a[2], x_order[2])
    weight_grad(3, 2)
    pass_a += scatter_pass(0, far_a[3], x_order[3])
    weight_grad(5, 1)
    big_ends = ([*near_a, *pass_a], [*near_b[1:], *pass_b], [*near_c, *pass_c])
    cs2, cs1 = [None] * 3, [None] * 3

    def middle(p):
        scatter_end(p, big_ends[p])
        cs2[p] = scatter_direct(p, 1)

    middle(2)
    weight_grad(6, 1)
    middle(1)
    middle(0)
    weight_grad(7, 1)

    view = final.at[core, me["x"]]
    q = [copy(view, view, dim, to) for dim, to in line_peers]
    settle(q)
    ended[me["y"], me["z"]] = sum(final[c, x] for c, x in eight)
    view = ended.at[me["y"], me["z"]]
    q = [copy(view, view, dim, to) for dim, to in plane_peers]
    for p in (2, 1, 0):
        settle(cs2[p])
        v = gview(p, 1, me[PARTS[p][2][1]], BOTH)
        v[...] = landed(r2, 3, p, 1).astype(bf16)
        cs1[p] = scatter_direct(p, 0)
    for p in (2, 1, 0):
        settle(cs1[p])
        off, w, _ = PARTS[p]
        gh_ref[:, off : off + w] = landed(r1, 3, p, 0).astype(bf16)
    settle(q)
    ending = sum(ended[y, z] for y in range(4) for z in range(4))
    token_loss = jnp.log(total) + top - ending[0:1]
    loss = jnp.sum(maskf * token_loss, keepdims=True) / denom
    squares = jnp.sum(ending[1:2, 0:128], keepdims=True)
    norm = jnp.sqrt(squares) / loss_scale
    clip = clip_limit / jnp.maximum(norm, clip_limit)
    two_ref[0:1, :] = jnp.broadcast_to(loss, (1, 128))
    two_ref[1:2, :] = jnp.broadcast_to(clip, (1, 128))
    for c in sent:
        c.wait_send()


def scaled(two_ref, gh_in, raw_ref, loss_ref, gh_out, out_ref, buf, sems):
    near = pltpu.make_async_copy(gh_in, gh_out, sems.at[8])
    near.start()
    clip = two_ref[1:2, 0:1]
    loss_ref[...] = two_ref[0:1, 0:1]
    copies = []
    for n in range(8):
        cols = slice(n * 512, (n + 1) * 512)
        buf[n] = (raw_ref[0:VOCAB, cols] * clip).astype(jnp.bfloat16)
        c = pltpu.make_async_copy(buf.at[n], out_ref.at[:, cols], sems.at[n])
        c.start()
        copies.append(c)
    near.wait()
    for c in copies:
        c.wait()


def step(hidden, weight, targets, mask, loss_scale):
    f32, bf16 = jnp.float32, jnp.bfloat16
    any_space = pl.BlockSpec(memory_space=pl.ANY)
    vmem = pl.BlockSpec(memory_space=pltpu.VMEM)
    smem = pl.BlockSpec(memory_space=pltpu.SMEM)
    V = pltpu.VMEM
    two, near, raw = pl.pallas_call(
        kernel,
        out_shape=(V((8, 128), f32), V((ROWS, WIDE), bf16), V((PAD, 4 * WIDE), f32)),
        grid=(1,),
        in_specs=[
            any_space, any_space, pl.BlockSpec((8, 4 * WIDE), lambda i: (EDGE // 8, 0)), vmem, vmem, smem,
        ],
        out_specs=(vmem, vmem, vmem),
        scratch_shapes=[
            V((2, 4, 2, 4, 4, 16, WIDE), bf16),
            V((PAD, 4 * WIDE), bf16),
            V((PAD, TOKENS), f32),
            V((PAD, TOKENS), bf16),
            V((TOKENS, PAD), bf16),
            V((4, 4, 4, ROWS, WIDE), bf16),
            V((4, 4, 4, ROWS, WIDE), bf16),
            V((4, 4, 4, ROWS, WIDE), bf16),
            V((2, 4, 4, 16, WIDE), bf16),
            V((2, 4, 4, ROWS, WIDE), bf16),
            V((3, 4, ROWS, WIDE), bf16),
            V((3, ROWS, WIDE), bf16),
            V((2, 4, 4, 8, 128), jnp.int32),
            V((2, 4, 2, 1, TOKENS), f32),
            V((4, 4, 2, 1, TOKENS), f32),
            V((2, 4, 2, TOKENS), f32),
            V((4, 4, 2, TOKENS), f32),
            pltpu.SemaphoreType.DMA((N_SEMS,)),
            pltpu.SemaphoreType.DMA((N_SEMS,)),
            pltpu.SemaphoreType.DMA((4,)),
        ],
        compiler_params=pltpu.CompilerParams(
            collective_id=0, has_side_effects=True, vmem_limit_bytes=95 * 512 * 1024
        ),
    )(hidden, weight.T, weight.T, targets.reshape(1, ROWS), mask.reshape(1, ROWS), loss_scale.reshape(1))
    loss, grad_hidden, grad_weight = pl.pallas_call(
        scaled,
        out_shape=(
            jax.ShapeDtypeStruct((1, 1), f32),
            jax.ShapeDtypeStruct((ROWS, WIDE), bf16),
            jax.ShapeDtypeStruct((VOCAB, 4 * WIDE), bf16),
        ),
        in_specs=[vmem, vmem, vmem],
        out_specs=(vmem, any_space, any_space),
        scratch_shapes=[V((8, VOCAB, 512), bf16), pltpu.SemaphoreType.DMA((9,))],
        compiler_params=pltpu.CompilerParams(vmem_limit_bytes=24 * 1024 * 1024),
    )(two, near, raw)
    return loss[0, 0], grad_hidden, grad_weight.T


def solution(mesh):
    torus = Mesh(
        mesh.devices.reshape(4, 4, 2, mesh.shape["tensor"]),
        ("context_0", "context_1", "context_2", "tensor"),
    )
    placed = (P(CONTEXT, "tensor"), P(None, CONTEXT_TENSOR), P(CONTEXT), P(CONTEXT), P())
    return jax.shard_map(
        step,
        mesh=torus,
        in_specs=placed,
        out_specs=(P(), P(CONTEXT, "tensor"), P(None, CONTEXT_TENSOR)),
        check_vma=False,
    )
```
